512 devices in a mesh: query: 16 (over y, x_lo), train: 16 (over x_hi, z), mp: 2 (over core).
Axes of the slice: x: 4 (x_hi: 2, x_lo: 2; x = x_hi * 2 + x_lo), y: 8, z: 8, core: 2. Of those that a mesh axis runs over, the one named last changes fastest.
Arguments:
- residual: bfloat16 [2048, 8192], P('train'), may hold values from -6 to 6
- norm_gain: float32 [8192], replicated, may hold values from 0.1 to 1.9
- gate_weight: bfloat16 [8192, 14336], P('train', ('query', 'mp')), may hold values from -0.0625 to 0.0625
- up_weight: bfloat16 [8192, 14336], P('train', ('query', 'mp')), may hold values from -0.0625 to 0.0625
- out_grad: bfloat16 [2048, 8192], P('train', ('query', 'mp')), may hold values from -6 to 6
- left_factor: bfloat16 [32, 32, 14336], P(('query', 'mp')), may hold values from -0.0078125 to 0.0078125
- right_factor: bfloat16 [32, 32, 8192], P(('query', 'mp')), may hold values from -0.0625 to 0.0625
Outputs:
- scores: float32 [32, 2048], P(('query', 'mp'), 'train')
The draws below stay inside these ranges and needn't reach their ends.
All inputs are finite; a program needn't handle non-finite values.
Results may differ from the reference program's by a relative error of at most 0.023.
Values may be sent and summed in bfloat16 or wider, within the bound.
No kernel may reach another device: no remote copies, remote signals or barrier semaphores. Data moves between devices by JAX's collectives and lax.ppermute only.
A program may use at most 64 MiB of HBM per device.

```python
import jax
import jax.numpy as jnp
from jax import lax

D = 8192
FF = 14336
R = 32
TOKENS = 2048
NQ = 32
N_TRAIN = 16


def level_of(rng, shape, cuts, least, top_value):
    gain, own = 1.0, jax.random.fold_in(rng, 6)
    for dim, shards_of in cuts:
        draws = jnp.exp(jax.random.uniform(jax.random.fold_in(own, dim), (shards_of,), jnp.float32, least / len(cuts), top_value / len(cuts)))
        gain = gain * jnp.repeat(draws, shape[dim] // shards_of).reshape([-1 if axis == dim else 1 for axis in range(len(shape))])
    return gain


def gaussian(stream_key, shape, deviation, bound, cuts=(), held_as=jnp.bfloat16):
    values = jax.random.normal(stream_key, shape, jnp.float32) * deviation
    if len(cuts) > 0:
        values = level_of(stream_key, shape, cuts, -0.22, 0.18) * values
    return jnp.clip(values, min=-bound, max=bound).astype(held_as)


def setup_inputs(seed: int = 0) -> dict:
    streams_of = jax.random.split(jax.random.key(seed), 8)
    return {
        "residual": gaussian(streams_of[0], (TOKENS, D), 1.0, 6.0, ((0, 16),)),
        "norm_gain": jnp.clip(1.0 + 0.18 * jax.random.normal(streams_of[1], (D,), jnp.float32), 0.1, 1.9),
        "gate_weight": gaussian(streams_of[2], (D, FF), D ** -0.5, 0.0625, ((0, 16), (1, 32))),
        "up_weight": gaussian(streams_of[3], (D, FF), D ** -0.5, 0.0625, ((0, 16), (1, 32))),
        "out_grad": gaussian(streams_of[4], (TOKENS, D), 1.0, 6.0, ((0, 16), (1, 32))),
        "left_factor": gaussian(streams_of[5], (NQ, R, FF), (FF * R) ** -0.5, 0.0078125, ((0, 32),)),
        "right_factor": gaussian(streams_of[6], (NQ, R, D), D ** -0.5, 0.0625, ((0, 32),)),
    }


norm_eps = 1e-05

def reference(residual, norm_gain, gate_weight, up_weight, out_grad, left_factor, right_factor):
    values = residual.astype(jnp.float32)
    mean_sq = lax.optimization_barrier(jnp.mean(values * values, axis=1, keepdims=True))
    normed = (values * lax.rsqrt(mean_sq + norm_eps) * norm_gain[None, :]).astype(jnp.bfloat16)
    block_rows = D // N_TRAIN
    normed_blocks = normed.reshape(TOKENS, N_TRAIN, block_rows).transpose(1, 0, 2)
    paired = jnp.concatenate([gate_weight, up_weight], axis=1).reshape(N_TRAIN, block_rows, 2 * FF)

    def add_block(running, pieces):
        row_block, weight_block = pieces
        term = jnp.dot(row_block, weight_block, preferred_element_type=jnp.float32).astype(jnp.bfloat16)
        term = lax.optimization_barrier(term).astype(jnp.float32)
        return (running + term, None)
    summed, unused = lax.scan(add_block, jnp.zeros((TOKENS, 2 * FF), jnp.float32), (normed_blocks, paired))
    activation = (jax.nn.silu(summed[:, :FF]) * summed[:, FF:]).astype(jnp.bfloat16)
    contract = (((1,), (1,)), ((), ()))
    projected = lax.dot_general(left_factor.reshape(NQ * R, FF), activation, contract, preferred_element_type=jnp.float32)
    sensed = lax.dot_general(right_factor.reshape(NQ * R, D), out_grad, contract, preferred_element_type=jnp.float32)
    return lax.optimization_barrier(jnp.sum((projected * sensed).reshape(NQ, R, TOKENS), axis=1))
```

```python
import functools

import jax
import jax.numpy as jnp
from jax import lax
from jax.experimental import pallas as pl
from jax.experimental.pallas import tpu as pltpu
from jax.sharding import Mesh
from jax.sharding import PartitionSpec as P

TRAIN = ("xh", "z")
QM = ("y", "xl", "c")
CHIPS = ("y", "xl")
SWAP = ((0, 1), (1, 0))

norm_eps = 1e-05


def norm_kernel(half_ref, res_ref, gain_ref, out_ref):
    values = res_ref[...].astype(jnp.float32)
    mean_sq = jnp.mean(values * values, axis=1, keepdims=True)
    scale = lax.rsqrt(mean_sq + norm_eps)
    peers, _, width = out_ref.shape
    rows = width // 2
    for xh in range(2):
        for k in range(peers):
            at = (xh * peers + k) * rows
            piece = res_ref[:, at : at + rows].astype(jnp.float32)
            piece = piece * scale * gain_ref[:, at : at + rows]
            out_ref[k, :, xh * rows : (xh + 1) * rows] = piece.astype(out_ref.dtype)


def normed_by_peer(residual, norm_gain, half, peers):
    tokens, width = residual.shape
    mine, slab = tokens // 2, 16
    steps = mine // slab
    return pl.pallas_call(
        norm_kernel,
        out_shape=jax.ShapeDtypeStruct((peers, mine, width // peers), jnp.bfloat16),
        grid_spec=pltpu.PrefetchScalarGridSpec(
            num_scalar_prefetch=1,
            grid=(steps,),
            in_specs=[
                pl.BlockSpec((slab, width), lambda i, h: (h[0] * steps + i, 0)),
                pl.BlockSpec((1, width), lambda i, h: (0, 0)),
            ],
            out_specs=pl.BlockSpec((peers, slab, width // peers), lambda i, h: (0, i, 0)),
        ),
        compiler_params=pltpu.CompilerParams(vmem_limit_bytes=32 << 20),
        cost_estimate=pl.CostEstimate(flops=4 * mine * width, bytes_accessed=4 * mine * width, transcendentals=mine),
        name="norm_rows",
    )(half.reshape(1), residual, norm_gain.reshape(1, width))


def both(own, other, index, dim):
    first = jnp.where(index == 0, own, other)
    second = jnp.where(index == 0, other, own)
    return jnp.concatenate([first, second], axis=dim)


def on_device(residual, norm_gain, gate_weight, up_weight, out_grad, left_factor, right_factor):
    c, xh = lax.axis_index("c"), lax.axis_index("xh")
    peers, chips = lax.axis_size("z"), lax.axis_size(CHIPS)
    tokens = residual.shape[0]
    half = tokens // 2
    cols = gate_weight.shape[1]
    rank = left_factor.shape[1]

    normed = normed_by_peer(residual, norm_gain, c, peers)
    rows = lax.all_to_all(normed, "z", 0, 0, tiled=True)
    rows_flat = rows.reshape(peers * half, -1)

    mine = jnp.concatenate([gate_weight.T, up_weight.T], axis=0)
    theirs = lax.ppermute(mine, "xh", SWAP)
    paired = both(mine, theirs, xh, 1)
    neighbour = lax.ppermute(paired, "c", SWAP)
    gate = both(paired[:cols], neighbour[:cols], c, 0)
    up = both(paired[cols:], neighbour[cols:], c, 0)
    weight = jnp.concatenate([gate, up], axis=0)

    contract = (((1,), (1,)), ((), ()))
    term = lax.dot_general(rows_flat, weight, contract, preferred_element_type=jnp.float32)
    term = term.astype(jnp.bfloat16).reshape(peers, half, -1)
    summed = lax.psum_scatter(term, "z", scatter_dimension=0, tiled=True)

    left = left_factor.reshape(rank, chips, -1)
    right = right_factor.reshape(rank, chips, -1)
    hidden = left.shape[2]
    packed = jnp.concatenate([left, right], axis=2).transpose(1, 0, 2)
    packed, rows = lax.optimization_barrier((packed, rows))
    got = lax.all_to_all(packed, CHIPS, 0, 0, tiled=True)
    beside = lax.ppermute(got, "c", SWAP)
    first = jnp.where(c == 0, got, beside)
    second = jnp.where(c == 0, beside, got)
    factors = jnp.stack([first, second], axis=1).reshape(chips * 2 * rank, -1)

    keep = lax.dynamic_slice_in_dim(out_grad, c * half, half, 0)
    give = lax.dynamic_slice_in_dim(out_grad, (1 - c) * half, half, 0)
    grad = both(keep, lax.ppermute(give, "c", SWAP), c, 1)
    sensed = lax.dot_general(factors[:, hidden:], grad, contract, preferred_element_type=jnp.float32)

    summed = summed[0].astype(jnp.float32)
    activation = (jax.nn.silu(summed[:, :hidden]) * summed[:, hidden:]).astype(jnp.bfloat16)
    projected = lax.dot_general(factors[:, :hidden], activation, contract, preferred_element_type=jnp.float32)

    parts = jnp.concatenate([projected, sensed], axis=1).astype(jnp.bfloat16)
    parts = parts.reshape(2 * chips, rank, 2 * half)
    parts = lax.all_to_all(parts, QM, 0, 0, tiled=True)
    whole = jnp.sum(parts.reshape(chips, 2, rank, 2 * half).astype(jnp.float32), axis=0)
    scores = jnp.sum(whole[:, :, :half] * whole[:, :, half:], axis=1)
    return scores.reshape(1, tokens)


def solution(mesh):
    torus = Mesh(mesh.devices.reshape(8, 2, 2, 8, 2), ("y", "xl", "xh", "z", "c"))
    placed = (
        P(TRAIN, None),
        P(),
        P(TRAIN, QM),
        P(TRAIN, QM),
        P(TRAIN, QM),
        P(QM, None, None),
        P(QM, None, None),
    )
    return jax.shard_map(on_device, mesh=torus, in_specs=placed, out_specs=P(QM, TRAIN), check_vma=False)
```

```python
import jax
import jax.numpy as jnp
from jax import lax
from jax.experimental import pallas as pl
from jax.experimental.pallas import tpu as pltpu
from jax.sharding import Mesh
from jax.sharding import PartitionSpec as P

TRAIN = ("xh", "z")
QM = ("y", "xl", "c")
CHIPS = ("y", "xl")
SWAP = ((0, 1), (1, 0))
RING = 8
STEPS = RING // 2 + 1
EARLY = (3, 2, 1)


def away(step, xh):
    sign = 1 if step % 2 else -1
    return step if step in (0, RING // 2) else sign * step * (1 - 2 * xh)


norm_eps = 1e-05


def norm_kernel(core_ref, pair_ref, own_ref, other_ref, own_gain_ref, other_gain_ref, out_ref):
    halves = [ref[...].astype(jnp.float32) for ref in (own_ref, other_ref)]
    gains = [ref[...] for ref in (own_gain_ref, other_gain_ref)]
    peers, _, width = out_ref.shape
    square = sum(jnp.sum(h * h, axis=1, keepdims=True) for h in halves)
    scale = lax.rsqrt(square / (peers * width) + norm_eps)
    rows = width // 2
    for part in range(2):
        normed = (halves[part] * scale * gains[part]).astype(out_ref.dtype)
        for k in range(peers):
            out_ref[k, :, part * rows : (part + 1) * rows] = normed[:, k * rows : (k + 1) * rows]


def normed_by_peer(residual, norm_gain, core, pair, peers):
    tokens, width = residual.shape
    mine, slab = tokens // 2, 32
    steps = mine // slab
    gain = norm_gain.reshape(1, width)
    return pl.pallas_call(
        norm_kernel,
        out_shape=jax.ShapeDtypeStruct((peers, mine, width // peers), jnp.bfloat16),
        grid_spec=pltpu.PrefetchScalarGridSpec(
            num_scalar_prefetch=2,
            grid=(steps,),
            in_specs=[
                pl.BlockSpec((slab, width // 2), lambda i, c, x: (c[0] * steps + i, x[0])),
                pl.BlockSpec((slab, width // 2), lambda i, c, x: (c[0] * steps + i, 1 - x[0])),
                pl.BlockSpec((1, width // 2), lambda i, c, x: (0, x[0])),
                pl.BlockSpec((1, width // 2), lambda i, c, x: (0, 1 - x[0])),
            ],
            out_specs=pl.BlockSpec((peers, slab, width // peers), lambda i, c, x: (0, i, 0)),
        ),
        compiler_params=pltpu.CompilerParams(vmem_limit_bytes=60 << 20),
        cost_estimate=pl.CostEstimate(flops=4 * mine * width, bytes_accessed=4 * mine * width, transcendentals=mine),
        name="norm_rows",
    )(core.reshape(1), pair.reshape(1), residual, residual, gain, gain)


def term_kernel(rows_ref, weight_ref, out_ref):
    peers, half, width = rows_ref.shape
    rows = rows_ref[...].reshape(peers * half, width)
    cols = weight_ref.shape[0] // 2
    for core in range(2):
        at = slice(core * cols, (core + 1) * cols)
        total = lax.dot_general(rows, weight_ref[at], (((1,), (1,)), ((), ())), preferred_element_type=jnp.float32)
        out_ref[:, :, at] = total.astype(out_ref.dtype).reshape(peers, half, cols)


def terms_of(rows, weight):
    peers, half, width = rows.shape
    cols = weight.shape[0]
    return pl.pallas_call(
        term_kernel,
        out_shape=jax.ShapeDtypeStruct((peers, half, cols), jnp.bfloat16),
        compiler_params=pltpu.CompilerParams(vmem_limit_bytes=24 << 20),
        cost_estimate=pl.CostEstimate(
            flops=2 * peers * half * width * cols, bytes_accessed=2 * cols * width + 6 * peers * half * width, transcendentals=0
        ),
        name="terms",
    )(rows, weight)


def whole_kernel(body, scalars, inputs, outputs, name):
    size = sum(v.size * v.dtype.itemsize for v in (*inputs, *outputs))
    vmem = pl.BlockSpec(memory_space=pltpu.VMEM)
    return pl.pallas_call(
        body,
        out_shape=outputs,
        in_specs=[pl.BlockSpec(memory_space=pltpu.SMEM)] * len(scalars) + [vmem] * len(inputs),
        out_specs=[vmem] * len(outputs),
        compiler_params=pltpu.CompilerParams(vmem_limit_bytes=24 << 20),
        cost_estimate=pl.CostEstimate(flops=0, bytes_accessed=size, transcendentals=0),
        name=name,
    )(*(v.reshape(1) for v in scalars), *inputs)


def weight_kernel(mine_ref, theirs_ref, beside_ref, across_ref, out_ref):
    cols, depth = mine_ref.shape
    for row, refs in enumerate(((mine_ref, theirs_ref), (beside_ref, across_ref))):
        for col, ref in enumerate(refs):
            out_ref[row * cols : (row + 1) * cols, col * depth : (col + 1) * depth] = ref[...]


def pack_kernel(y_ref, xh_ref, left_ref, right_ref, *out_refs):
    rank, hidden = left_ref.shape[0], left_ref.shape[1] // (2 * RING)
    features = right_ref.shape[1] // (2 * RING)
    for step, out_ref in enumerate(out_refs):
        to = lax.rem(y_ref[0] + RING + away(step, xh_ref[0]), RING)
        for xl in range(2):
            at = pl.multiple_of((to * 2 + xl) * hidden, 128)
            out_ref[xl, :, :hidden] = left_ref[:, pl.ds(at, hidden)]
            at = pl.multiple_of((to * 2 + xl) * features, 128)
            out_ref[xl, :, hidden:] = right_ref[:, pl.ds(at, features)]


def give_kernel(xl_ref, *refs):
    arrived, (aside_ref, across_ref, apart_ref) = refs[:-3], refs[-3:]
    xl = xl_ref[0]
    for step, ref in enumerate(arrived):
        aside_ref[step] = ref[1 - xl]
        if step > 0:
            across_ref[step - 1] = ref[xl]
            apart_ref[step - 1] = ref[1 - xl]


def gather_kernel(c_ref, xl_ref, y_ref, xh_ref, *refs):
    arrived, refs = refs[:STEPS], refs[STEPS:]
    aside_ref, far_ref, across_ref, apart_ref, grad_ref, beside_ref, left_ref, sensed_ref, right_ref = refs
    hidden = left_ref.shape[-1]
    xl = xl_ref[0]
    for step, ref in enumerate(arrived):
        source = lax.rem(y_ref[0] + RING - away(step, xh_ref[0]), RING)
        found = [(source, xl, ref[xl]), (source, 1 - xl, (aside_ref[step] if step < STEPS - 1 else far_ref[...]))]
        if 0 < step < STEPS - 1:
            source = lax.rem(y_ref[0] + RING + away(step, xh_ref[0]), RING)
            found += [(source, xl, across_ref[step - 1]), (source, 1 - xl, apart_ref[step - 1])]
        for source, at, value in found:
            left_ref[source, at] = value[:, :hidden]
            right_ref[source, at] = value[:, hidden:]
    ring, _, rank, features = right_ref.shape
    total = jnp.zeros(sensed_ref.shape, jnp.float32)
    for core, ref in ((c_ref[0], grad_ref), (1 - c_ref[0], beside_ref)):
        at = pl.ds(pl.multiple_of(core * (features // 2), 128), features // 2)
        factor = right_ref[:, :, :, at].reshape(2 * ring * rank, features // 2)
        total += lax.dot_general(factor, ref[...], (((1,), (1,)), ((), ())), preferred_element_type=jnp.float32)
    sensed_ref[...] = total.astype(sensed_ref.dtype)


def in_order(own, other, index, dim):
    return jnp.concatenate([jnp.where(index == 0, own, other), jnp.where(index == 0, other, own)], axis=dim)


def on_device(residual, norm_gain, gate_weight, up_weight, out_grad, left_factor, right_factor):
    c, xh, xl, y = (lax.axis_index(name) for name in ("c", "xh", "xl", "y"))
    peers, chips = lax.axis_size("z"), lax.axis_size(CHIPS)
    tokens = residual.shape[0]
    cols = gate_weight.shape[1]
    rank = left_factor.shape[1]
    hidden, features = left_factor.shape[2] // chips, right_factor.shape[2] // chips
    packed = hidden + features
    always = c >= 0

    def fenced(work, *inputs):
        shapes = jax.eval_shape(work, *inputs)
        return lax.cond(always, work, lambda *_: jax.tree.map(lambda s: jnp.zeros(s.shape, s.dtype), shapes), *inputs)

    def like(*shape):
        return jax.ShapeDtypeStruct(shape, jnp.bfloat16)

    def along_y(piece, step):
        pairs = [(i * 2 + h, (i + RING + away(step, h)) % RING * 2 + h) for i in range(RING) for h in range(2)]
        return lax.ppermute(piece, ("y", "xh"), pairs)

    def beside_tokens(gate_weight, up_weight, out_grad, left_factor, right_factor):
        mine = jnp.concatenate([gate_weight.T, up_weight.T], axis=0)
        theirs = lax.ppermute(mine, "xh", SWAP)
        pieces = whole_kernel(
            pack_kernel, (y, xh), (left_factor[0], right_factor[0]), [like(2, rank, packed)] * STEPS, "pack_factors"
        )
        early = tuple(along_y(pieces[step], step) for step in EARLY)
        theirs, early = lax.optimization_barrier((theirs, early))
        beside = (lax.ppermute(mine, "c", SWAP), lax.ppermute(theirs, "c", SWAP))
        (weight,) = whole_kernel(
            weight_kernel, (), (mine, theirs, *beside), [like(4 * cols, 2 * gate_weight.shape[0])], "weights"
        )
        late = (pieces[0], pieces[STEPS - 1])
        return weight, early, late, lax.ppermute(out_grad, "c", SWAP)

    def beside_sums(early, late, out_grad, beside_grad):
        far = along_y(late[1], STEPS - 1)
        near = [late[0]] + [early[EARLY.index(step)] for step in range(1, STEPS - 1)]
        pieces = [like(STEPS - 1, rank, packed)] + [like(STEPS - 2, rank, packed)] * 2
        aside, across, apart = whole_kernel(give_kernel, (xl,), near, pieces, "give")
        across = lax.ppermute(across, "xh", SWAP)
        apart = lax.ppermute(apart, ("xl", "xh"), [(i, 3 - i) for i in range(4)])
        aside = lax.ppermute(aside, "xl", SWAP)
        beyond = lax.ppermute(lax.dynamic_index_in_dim(far, 1 - xl, 0, keepdims=False), "xl", SWAP)
        outputs = [like(RING, 2, rank, hidden), like(chips * rank, tokens), like(RING, 2, rank, features)]
        inputs = (*near, far, aside, beyond, across, apart, out_grad, beside_grad)
        left, sensed, _ = whole_kernel(gather_kernel, (c, xl, y, xh), inputs, outputs, "gather_factors")
        return left.reshape(chips * rank, hidden), sensed

    normed = normed_by_peer(residual, norm_gain, c, xh, peers)
    inputs, normed = lax.optimization_barrier(((gate_weight, up_weight, out_grad, left_factor, right_factor), normed))
    rows = lax.all_to_all(normed, "z", 0, 0, tiled=True)
    weight, early, late, beside_grad = fenced(beside_tokens, *inputs)

    term = terms_of(rows, weight)
    inputs, term = lax.optimization_barrier(((early, late, out_grad, beside_grad), term))
    summed = lax.all_to_all(term, "z", 0, 0, tiled=True)
    factors, sensed = fenced(beside_sums, *inputs)

    summed = jnp.sum(summed.astype(jnp.float32), axis=0)
    active = [
        (jax.nn.silu(summed[:, at : at + cols]) * summed[:, at + cols : at + 2 * cols]).astype(jnp.bfloat16)
        for at in (0, 2 * cols)
    ]
    active = in_order(*active, c, 1)
    active, factors, sensed = lax.optimization_barrier((active, factors, sensed))
    active = in_order(active, lax.ppermute(active, "c", SWAP), c, 0)
    projected = lax.dot_general(factors, active, (((1,), (1,)), ((), ())), preferred_element_type=jnp.float32)

    parts = [v.reshape(chips, rank, tokens) for v in (projected.astype(jnp.bfloat16), sensed)]
    parts = lax.all_to_all(jnp.concatenate(parts, axis=1), CHIPS, 0, 0, tiled=True)
    whole = jnp.sum(parts.astype(jnp.float32), axis=0)
    return jnp.sum(whole[:rank] * whole[rank:], axis=0, keepdims=True)


def solution(mesh):
    torus = Mesh(mesh.devices.reshape(8, 2, 2, 8, 2), ("y", "xl", "xh", "z", "c"))
    placed = (
        P(TRAIN, None),
        P(),
        P(TRAIN, QM),
        P(TRAIN, QM),
        P(TRAIN, QM),
        P(QM, None, None),
        P(QM, None, None),
    )
    return jax.shard_map(on_device, mesh=torus, in_specs=placed, out_specs=P(QM, TRAIN), check_vma=False)
```

```python
import jax
import jax.numpy as jnp
from jax import lax
from jax.experimental import pallas as pl
from jax.experimental.pallas import tpu as pltpu
from jax.sharding import Mesh
from jax.sharding import PartitionSpec as P

TRAIN = ("xh", "zh", "zl")
DEPTH = ("zh", "zl")
QM = ("y", "xl", "c")
CHIPS = ("y", "xl")
SWAP = ((0, 1), (1, 0))
RING = 8
STEPS = RING // 2 + 1
EARLY = (3, 2, 1)


def away(step, xh):
    sign = 1 if step == 3 else -1
    return step if step in (0, RING // 2) else sign * step * (1 - 2 * xh)


norm_eps = 1e-05


def norm_kernel(core_ref, pair_ref, own_ref, other_ref, own_gain_ref, other_gain_ref, out_ref):
    halves = [ref[...].astype(jnp.float32) for ref in (own_ref, other_ref)]
    gains = [ref[...] for ref in (own_gain_ref, other_gain_ref)]
    peers, _, width = out_ref.shape
    square = sum(jnp.sum(h * h, axis=1, keepdims=True) for h in halves)
    scale = lax.rsqrt(square / (peers * width) + norm_eps)
    rows = width // 2
    for part in range(2):
        normed = (halves[part] * scale * gains[part]).astype(out_ref.dtype)
        for k in range(peers):
            out_ref[k, :, part * rows : (part + 1) * rows] = normed[:, k * rows : (k + 1) * rows]


def normed_by_peer(residual, norm_gain, core, pair, peers):
    tokens, width = residual.shape
    mine, slab = tokens // 2, 32
    steps = mine // slab
    gain = norm_gain.reshape(1, width)
    return pl.pallas_call(
        norm_kernel,
        out_shape=jax.ShapeDtypeStruct((peers, mine, width // peers), jnp.bfloat16),
        grid_spec=pltpu.PrefetchScalarGridSpec(
            num_scalar_prefetch=2,
            grid=(steps,),
            in_specs=[
                pl.BlockSpec((slab, width // 2), lambda i, c, x: (c[0] * steps + i, x[0])),
                pl.BlockSpec((slab, width // 2), lambda i, c, x: (c[0] * steps + i, 1 - x[0])),
                pl.BlockSpec((1, width // 2), lambda i, c, x: (0, x[0])),
                pl.BlockSpec((1, width // 2), lambda i, c, x: (0, 1 - x[0])),
            ],
            out_specs=pl.BlockSpec((peers, slab, width // peers), lambda i, c, x: (0, i, 0)),
        ),
        compiler_params=pltpu.CompilerParams(vmem_limit_bytes=60 << 20),
        cost_estimate=pl.CostEstimate(flops=4 * mine * width, bytes_accessed=4 * mine * width, transcendentals=mine),
        name="norm_rows",
    )(core.reshape(1), pair.reshape(1), residual, residual, gain, gain)


def term_kernel(parity_ref, rows_ref, weight_ref, *out_refs):
    peers, half, width = rows_ref.shape
    rows = jnp.concatenate([rows_ref[2 * i + parity_ref[0]] for i in range(peers // 2)], axis=0)
    cols = weight_ref.shape[0] // 2
    for core, out_ref in enumerate(out_refs):
        weight = weight_ref[core * cols : (core + 1) * cols]
        total = lax.dot_general(rows, weight, (((1,), (1,)), ((), ())), preferred_element_type=jnp.float32)
        out_ref[...] = total.astype(out_ref.dtype).reshape(out_ref.shape)


def terms_of(rows, weight, parity, kind):
    peers, half, width = rows.shape
    cols = weight.shape[0]
    shape = jax.ShapeDtypeStruct((peers // 2, half, cols // 2), kind)
    return whole_kernel(term_kernel, (parity,), (rows, weight), [shape] * 2, "terms", peers * half * width * cols)


def add_kernel(keep_ref, beside_ref, got_ref, across_ref, out_ref):
    cols = keep_ref.shape[2]
    for at, (own, other) in enumerate(((keep_ref, got_ref), (beside_ref, across_ref))):
        total = own[...] + other[...].astype(jnp.float32)
        out_ref[:, :, at * cols : (at + 1) * cols] = total.astype(out_ref.dtype)


def whole_kernel(body, scalars, inputs, outputs, name, flops=0):
    size = sum(v.size * v.dtype.itemsize for v in (*inputs, *outputs))
    vmem = pl.BlockSpec(memory_space=pltpu.VMEM)
    return pl.pallas_call(
        body,
        out_shape=outputs,
        in_specs=[pl.BlockSpec(memory_space=pltpu.SMEM)] * len(scalars) + [vmem] * len(inputs),
        out_specs=[vmem] * len(outputs),
        compiler_params=pltpu.CompilerParams(vmem_limit_bytes=24 << 20),
        cost_estimate=pl.CostEstimate(flops=flops, bytes_accessed=size, transcendentals=0),
        name=name,
    )(*(v.reshape(1) for v in scalars), *inputs)


def weight_kernel(mine_ref, theirs_ref, beside_ref, across_ref, out_ref):
    cols, depth = mine_ref.shape
    for row, refs in enumerate(((mine_ref, theirs_ref), (beside_ref, across_ref))):
        for col, ref in enumerate(refs):
            out_ref[row * cols : (row + 1) * cols, col * depth : (col + 1) * depth] = ref[...]


def pack_kernel(y_ref, xh_ref, left_ref, right_ref, *out_refs):
    rank, hidden = left_ref.shape[0], left_ref.shape[1] // (2 * RING)
    features = right_ref.shape[1] // (2 * RING)
    for step, out_ref in enumerate(out_refs):
        to = lax.rem(y_ref[0] + RING + away(step, xh_ref[0]), RING)
        for xl in range(2):
            at = pl.multiple_of((to * 2 + xl) * hidden, 128)
            out_ref[xl, :, :hidden] = left_ref[:, pl.ds(at, hidden)]
            at = pl.multiple_of((to * 2 + xl) * features, 128)
            out_ref[xl, :, hidden:] = right_ref[:, pl.ds(at, features)]


def give_kernel(xl_ref, *refs):
    arrived, (aside_ref, across_ref, apart_ref) = refs[:-3], refs[-3:]
    xl = xl_ref[0]
    for step, ref in enumerate(arrived):
        aside_ref[step] = ref[1 - xl]
        if step > 0:
            across_ref[step - 1] = ref[xl]
            apart_ref[step - 1] = ref[1 - xl]


def gather_kernel(c_ref, xl_ref, y_ref, xh_ref, *refs):
    arrived, refs = refs[:STEPS], refs[STEPS:]
    aside_ref, far_ref, across_ref, apart_ref, grad_ref, beside_ref, left_ref, sensed_ref, right_ref = refs
    hidden = left_ref.shape[-1]
    xl = xl_ref[0]
    for step, ref in enumerate(arrived):
        source = lax.rem(y_ref[0] + RING - away(step, xh_ref[0]), RING)
        found = [(source, xl, ref[xl]), (source, 1 - xl, (aside_ref[step] if step < STEPS - 1 else far_ref[...]))]
        if 0 < step < STEPS - 1:
            source = lax.rem(y_ref[0] + RING + away(step, xh_ref[0]), RING)
            found += [(source, xl, across_ref[step - 1]), (source, 1 - xl, apart_ref[step - 1])]
        for source, at, value in found:
            left_ref[source, at] = value[:, :hidden]
            right_ref[source, at] = value[:, hidden:]
    ring, _, rank, features = right_ref.shape
    total = jnp.zeros(sensed_ref.shape, jnp.float32)
    for core, ref in ((c_ref[0], grad_ref), (1 - c_ref[0], beside_ref)):
        at = pl.ds(pl.multiple_of(core * (features // 2), 128), features // 2)
        factor = right_ref[:, :, :, at].reshape(2 * ring * rank, features // 2)
        total += lax.dot_general(factor, ref[...], (((1,), (1,)), ((), ())), preferred_element_type=jnp.float32)
    sensed_ref[...] = total.astype(sensed_ref.dtype)


def in_order(own, other, index, dim):
    return jnp.concatenate([jnp.where(index == 0, own, other), jnp.where(index == 0, other, own)], axis=dim)


def on_device(residual, norm_gain, gate_weight, up_weight, out_grad, left_factor, right_factor):
    c, xh, xl, y, zl = (lax.axis_index(name) for name in ("c", "xh", "xl", "y", "zl"))
    peers, chips = lax.axis_size(DEPTH), lax.axis_size(CHIPS)
    tokens = residual.shape[0]
    cols = gate_weight.shape[1]
    rank = left_factor.shape[1]
    hidden, features = left_factor.shape[2] // chips, right_factor.shape[2] // chips
    packed = hidden + features
    always = c >= 0

    def fenced(work, *inputs):
        shapes = jax.eval_shape(work, *inputs)
        return lax.cond(always, work, lambda *_: jax.tree.map(lambda s: jnp.zeros(s.shape, s.dtype), shapes), *inputs)

    def like(*shape):
        return jax.ShapeDtypeStruct(shape, jnp.bfloat16)

    def along_y(piece, step):
        pairs = [(i * 2 + h, (i + RING + away(step, h)) % RING * 2 + h) for i in range(RING) for h in range(2)]
        return lax.ppermute(piece, ("y", "xh"), pairs)

    def beside_tokens(gate_weight, up_weight, out_grad, left_factor, right_factor):
        mine = jnp.concatenate([gate_weight.T, up_weight.T], axis=0)
        theirs = lax.ppermute(mine, "xh", SWAP)
        pieces = whole_kernel(
            pack_kernel, (y, xh), (left_factor[0], right_factor[0]), [like(2, rank, packed)] * STEPS, "pack_factors"
        )
        early = tuple(along_y(pieces[step], step) for step in EARLY)
        theirs, early = lax.optimization_barrier((theirs, early))
        beside = (lax.ppermute(mine, "c", SWAP), lax.ppermute(theirs, "c", SWAP))
        (weight,) = whole_kernel(
            weight_kernel, (), (mine, theirs, *beside), [like(4 * cols, 2 * gate_weight.shape[0])], "weights"
        )
        late = (pieces[0], pieces[STEPS - 1])
        return weight, early, late, lax.ppermute(out_grad, "c", SWAP)

    def beside_sums(near, far, out_grad, beside_grad):
        pieces = [like(STEPS - 1, rank, packed)] + [like(STEPS - 2, rank, packed)] * 2
        aside, across, apart = whole_kernel(give_kernel, (xl,), near, pieces, "give")
        across = lax.ppermute(across, "xh", SWAP)
        apart = lax.ppermute(apart, ("xl", "xh"), [(i, 3 - i) for i in range(4)])
        aside = lax.ppermute(aside, "xl", SWAP)
        beyond = lax.ppermute(lax.dynamic_index_in_dim(far, 1 - xl, 0, keepdims=False), "xl", SWAP)
        outputs = [like(RING, 2, rank, hidden), like(chips * rank, tokens), like(RING, 2, rank, features)]
        inputs = (*near, far, aside, beyond, across, apart, out_grad, beside_grad)
        left, sensed, _ = whole_kernel(gather_kernel, (c, xl, y, xh), inputs, outputs, "gather_factors")
        return left.reshape(chips * rank, hidden), sensed

    normed = normed_by_peer(residual, norm_gain, c, xh, peers)
    inputs, normed = lax.optimization_barrier(((gate_weight, up_weight, out_grad, left_factor, right_factor), normed))
    rows = lax.all_to_all(normed, DEPTH, 0, 0, tiled=True)
    weight, early, late, beside_grad = fenced(beside_tokens, *inputs)

    give = terms_of(rows, weight, 1 - zl, jnp.bfloat16)
    give, rows = lax.optimization_barrier((give, rows))
    got = lax.ppermute(give[0], "zl", SWAP)
    across = lax.ppermute(give[1], DEPTH, [(i, (i + (1 if i % 2 else -1)) % peers) for i in range(peers)])
    keep = terms_of(rows, weight, zl, jnp.float32)
    late, give = lax.optimization_barrier((late, give))
    far = along_y(late[1], STEPS - 1)
    near = [late[0]] + [early[EARLY.index(step)] for step in range(1, STEPS - 1)]
    (term,) = whole_kernel(add_kernel, (), (*keep, got, across), [like(peers // 2, tokens // 2, 4 * cols)], "add_terms")
    inputs, term = lax.optimization_barrier(((near, far, out_grad, beside_grad), term))
    summed = lax.all_to_all(term, "zh", 0, 0, tiled=True)
    factors, sensed = fenced(beside_sums, *inputs)

    summed = jnp.sum(summed.astype(jnp.float32), axis=0)
    active = [
        (jax.nn.silu(summed[:, at : at + cols]) * summed[:, at + cols : at + 2 * cols]).astype(jnp.bfloat16)
        for at in (0, 2 * cols)
    ]
    active = in_order(*active, c, 1)
    active, factors, sensed = lax.optimization_barrier((active, factors, sensed))
    active = in_order(active, lax.ppermute(active, "c", SWAP), c, 0)
    projected = lax.dot_general(factors, active, (((1,), (1,)), ((), ())), preferred_element_type=jnp.float32)

    parts = [v.reshape(chips, rank, tokens) for v in (projected.astype(jnp.bfloat16), sensed)]
    parts = lax.all_to_all(jnp.concatenate(parts, axis=1), CHIPS, 0, 0, tiled=True)
    whole = jnp.sum(parts.astype(jnp.float32), axis=0)
    return jnp.sum(whole[:rank] * whole[rank:], axis=0, keepdims=True)


def solution(mesh):
    torus = Mesh(mesh.devices.reshape(8, 2, 2, 4, 2, 2), ("y", "xl", "xh", "zh", "zl", "c"))
    placed = (
        P(TRAIN, None),
        P(),
        P(TRAIN, QM),
        P(TRAIN, QM),
        P(TRAIN, QM),
        P(QM, None, None),
        P(QM, None, None),
    )
    return jax.shard_map(on_device, mesh=torus, in_specs=placed, out_specs=P(QM, TRAIN), check_vma=False)
```

```python
import jax
import jax.numpy as jnp
from jax import lax
from jax.experimental import pallas as pl
from jax.experimental.pallas import tpu as pltpu
from jax.sharding import Mesh
from jax.sharding import PartitionSpec as P

TRAIN = ("xh", "zh", "zl")
DEPTH = ("zh", "zl")
QM = ("y", "xl", "c")
CHIPS = ("y", "xl")
SWAP = ((0, 1), (1, 0))
RING = 8
STEPS = RING // 2 + 1
EARLY = (3, 2, 1)


def away(step, xh):
    sign = 1 if step == 3 else -1
    return step if step in (0, RING // 2) else sign * step * (1 - 2 * xh)


norm_eps = 1e-05


def norm_kernel(core_ref, pair_ref, own_ref, other_ref, own_gain_ref, other_gain_ref, out_ref):
    halves = [ref[...].astype(jnp.float32) for ref in (own_ref, other_ref)]
    gains = [ref[...] for ref in (own_gain_ref, other_gain_ref)]
    peers, _, width = out_ref.shape
    square = sum(jnp.sum(h * h, axis=1, keepdims=True) for h in halves)
    scale = lax.rsqrt(square / (peers * width) + norm_eps)
    rows = width // 2
    for part in range(2):
        normed = (halves[part] * scale * gains[part]).astype(out_ref.dtype)
        for k in range(peers):
            out_ref[k, :, part * rows : (part + 1) * rows] = normed[:, k * rows : (k + 1) * rows]


def normed_by_peer(residual, norm_gain, core, pair, peers):
    tokens, width = residual.shape
    mine, slab = tokens // 2, 32
    steps = mine // slab
    gain = norm_gain.reshape(1, width)
    return pl.pallas_call(
        norm_kernel,
        out_shape=jax.ShapeDtypeStruct((peers, mine, width // peers), jnp.bfloat16),
        grid_spec=pltpu.PrefetchScalarGridSpec(
            num_scalar_prefetch=2,
            grid=(steps,),
            in_specs=[
                pl.BlockSpec((slab, width // 2), lambda i, c, x: (c[0] * steps + i, x[0])),
                pl.BlockSpec((slab, width // 2), lambda i, c, x: (c[0] * steps + i, 1 - x[0])),
                pl.BlockSpec((1, width // 2), lambda i, c, x: (0, x[0])),
                pl.BlockSpec((1, width // 2), lambda i, c, x: (0, 1 - x[0])),
            ],
            out_specs=pl.BlockSpec((peers, slab, width // peers), lambda i, c, x: (0, i, 0)),
        ),
        compiler_params=pltpu.CompilerParams(vmem_limit_bytes=60 << 20),
        cost_estimate=pl.CostEstimate(flops=4 * mine * width, bytes_accessed=4 * mine * width, transcendentals=mine),
        name="norm_rows",
    )(core.reshape(1), pair.reshape(1), residual, residual, gain, gain)


def term_kernel(parity_ref, rows_ref, weight_ref, out_ref):
    peers, half, width = rows_ref.shape
    rows = jnp.concatenate([rows_ref[2 * i + parity_ref[0]] for i in range(peers // 2)], axis=0)
    cols = weight_ref.shape[0] // 2
    for core in range(2):
        at = slice(core * cols, (core + 1) * cols)
        total = lax.dot_general(rows, weight_ref[at], (((1,), (1,)), ((), ())), preferred_element_type=jnp.float32)
        out_ref[:, :, at] = total.astype(out_ref.dtype).reshape(peers // 2, half, cols)


def terms_of(rows, weight, parity, kind):
    peers, half, width = rows.shape
    cols = weight.shape[0]
    shape = jax.ShapeDtypeStruct((peers // 2, half, cols), kind)
    return whole_kernel(term_kernel, (parity,), (rows, weight), [shape], "terms", peers * half * width * cols)[0]


def add_kernel(keep_ref, got_ref, out_ref):
    out_ref[...] = (keep_ref[...] + got_ref[...].astype(jnp.float32)).astype(out_ref.dtype)


def whole_kernel(body, scalars, inputs, outputs, name, flops=0):
    size = sum(v.size * v.dtype.itemsize for v in (*inputs, *outputs))
    vmem = pl.BlockSpec(memory_space=pltpu.VMEM)
    return pl.pallas_call(
        body,
        out_shape=outputs,
        in_specs=[pl.BlockSpec(memory_space=pltpu.SMEM)] * len(scalars) + [vmem] * len(inputs),
        out_specs=[vmem] * len(outputs),
        compiler_params=pltpu.CompilerParams(vmem_limit_bytes=24 << 20),
        cost_estimate=pl.CostEstimate(flops=flops, bytes_accessed=size, transcendentals=0),
        name=name,
    )(*(v.reshape(1) for v in scalars), *inputs)


def weight_kernel(mine_ref, theirs_ref, beside_ref, across_ref, out_ref):
    cols, depth = mine_ref.shape
    for row, refs in enumerate(((mine_ref, theirs_ref), (beside_ref, across_ref))):
        for col, ref in enumerate(refs):
            out_ref[row * cols : (row + 1) * cols, col * depth : (col + 1) * depth] = ref[...]


def pack_kernel(y_ref, xh_ref, left_ref, right_ref, *out_refs):
    rank, hidden = left_ref.shape[0], left_ref.shape[1] // (2 * RING)
    features = right_ref.shape[1] // (2 * RING)
    for step, out_ref in enumerate(out_refs):
        to = lax.rem(y_ref[0] + RING + away(step, xh_ref[0]), RING)
        for xl in range(2):
            at = pl.multiple_of((to * 2 + xl) * hidden, 128)
            out_ref[xl, :, :hidden] = left_ref[:, pl.ds(at, hidden)]
            at = pl.multiple_of((to * 2 + xl) * features, 128)
            out_ref[xl, :, hidden:] = right_ref[:, pl.ds(at, features)]


def give_kernel(xl_ref, *refs):
    arrived, (aside_ref, across_ref, apart_ref) = refs[:-3], refs[-3:]
    xl = xl_ref[0]
    for step, ref in enumerate(arrived):
        aside_ref[step] = ref[1 - xl]
        if step > 0:
            across_ref[step - 1] = ref[xl]
            apart_ref[step - 1] = ref[1 - xl]


def gather_kernel(c_ref, xl_ref, y_ref, xh_ref, *refs):
    arrived, refs = refs[:STEPS], refs[STEPS:]
    aside_ref, far_ref, across_ref, apart_ref, grad_ref, beside_ref, left_ref, sensed_ref, right_ref = refs
    hidden = left_ref.shape[-1]
    xl = xl_ref[0]
    for step, ref in enumerate(arrived):
        source = lax.rem(y_ref[0] + RING - away(step, xh_ref[0]), RING)
        found = [(source, xl, ref[xl]), (source, 1 - xl, (aside_ref[step] if step < STEPS - 1 else far_ref[...]))]
        if 0 < step < STEPS - 1:
            source = lax.rem(y_ref[0] + RING + away(step, xh_ref[0]), RING)
            found += [(source, xl, across_ref[step - 1]), (source, 1 - xl, apart_ref[step - 1])]
        for source, at, value in found:
            left_ref[source, at] = value[:, :hidden]
            right_ref[source, at] = value[:, hidden:]
    ring, _, rank, features = right_ref.shape
    total = jnp.zeros(sensed_ref.shape, jnp.float32)
    for core, ref in ((c_ref[0], grad_ref), (1 - c_ref[0], beside_ref)):
        at = pl.ds(pl.multiple_of(core * (features // 2), 128), features // 2)
        factor = right_ref[:, :, :, at].reshape(2 * ring * rank, features // 2)
        total += lax.dot_general(factor, ref[...], (((1,), (1,)), ((), ())), preferred_element_type=jnp.float32)
    sensed_ref[...] = total.astype(sensed_ref.dtype)


def in_order(own, other, index, dim):
    return jnp.concatenate([jnp.where(index == 0, own, other), jnp.where(index == 0, other, own)], axis=dim)


def on_device(residual, norm_gain, gate_weight, up_weight, out_grad, left_factor, right_factor):
    c, xh, xl, y, zl = (lax.axis_index(name) for name in ("c", "xh", "xl", "y", "zl"))
    peers, chips = lax.axis_size(DEPTH), lax.axis_size(CHIPS)
    tokens = residual.shape[0]
    cols = gate_weight.shape[1]
    rank = left_factor.shape[1]
    hidden, features = left_factor.shape[2] // chips, right_factor.shape[2] // chips
    packed = hidden + features
    always = c >= 0

    def fenced(work, *inputs):
        shapes = jax.eval_shape(work, *inputs)
        return lax.cond(always, work, lambda *_: jax.tree.map(lambda s: jnp.zeros(s.shape, s.dtype), shapes), *inputs)

    def like(*shape):
        return jax.ShapeDtypeStruct(shape, jnp.bfloat16)

    def along_y(piece, step):
        pairs = [(i * 2 + h, (i + RING + away(step, h)) % RING * 2 + h) for i in range(RING) for h in range(2)]
        return lax.ppermute(piece, ("y", "xh"), pairs)

    def beside_tokens(gate_weight, up_weight, out_grad, left_factor, right_factor):
        mine = jnp.concatenate([gate_weight.T, up_weight.T], axis=0)
        theirs = lax.ppermute(mine, "xh", SWAP)
        pieces = whole_kernel(
            pack_kernel, (y, xh), (left_factor[0], right_factor[0]), [like(2, rank, packed)] * STEPS, "pack_factors"
        )
        early = tuple(along_y(pieces[step], step) for step in EARLY)
        theirs, early = lax.optimization_barrier((theirs, early))
        beside = (lax.ppermute(mine, "c", SWAP), lax.ppermute(theirs, "c", SWAP))
        (weight,) = whole_kernel(
            weight_kernel, (), (mine, theirs, *beside), [like(4 * cols, 2 * gate_weight.shape[0])], "weights"
        )
        late = (pieces[0], pieces[STEPS - 1])
        return weight, early, late, lax.ppermute(out_grad, "c", SWAP)

    def beside_sums(near, far, out_grad, beside_grad):
        pieces = [like(STEPS - 1, rank, packed)] + [like(STEPS - 2, rank, packed)] * 2
        aside, across, apart = whole_kernel(give_kernel, (xl,), near, pieces, "give")
        across = lax.ppermute(across, "xh", SWAP)
        apart = lax.ppermute(apart, ("xl", "xh"), [(i, 3 - i) for i in range(4)])
        aside = lax.ppermute(aside, "xl", SWAP)
        beyond = lax.ppermute(lax.dynamic_index_in_dim(far, 1 - xl, 0, keepdims=False), "xl", SWAP)
        outputs = [like(RING, 2, rank, hidden), like(chips * rank, tokens), like(RING, 2, rank, features)]
        inputs = (*near, far, aside, beyond, across, apart, out_grad, beside_grad)
        left, sensed, _ = whole_kernel(gather_kernel, (c, xl, y, xh), inputs, outputs, "gather_factors")
        return left.reshape(chips * rank, hidden), sensed

    normed = normed_by_peer(residual, norm_gain, c, xh, peers)
    inputs, normed = lax.optimization_barrier(((gate_weight, up_weight, out_grad, left_factor, right_factor), normed))
    rows = lax.all_to_all(normed, DEPTH, 0, 0, tiled=True)
    weight, early, late, beside_grad = fenced(beside_tokens, *inputs)

    give = terms_of(rows, weight, 1 - zl, jnp.bfloat16)
    give, rows = lax.optimization_barrier((give, rows))
    pairs = []
    for z in range(peers):
        for core in range(2):
            side = 1 if z % 2 == core else -1
            pairs.append((z * 2 + core, (z + side) % peers * 2 + core))
    got = lax.ppermute(give, DEPTH + ("c",), pairs)
    keep = terms_of(rows, weight, zl, jnp.float32)
    late, give = lax.optimization_barrier((late, give))
    far = along_y(late[1], STEPS - 1)
    near = [late[0]] + [early[EARLY.index(step)] for step in range(1, STEPS - 1)]
    (term,) = whole_kernel(add_kernel, (), (keep, got), [like(peers // 2, tokens // 2, 4 * cols)], "add_terms")
    inputs, term = lax.optimization_barrier(((near, far, out_grad, beside_grad), term))
    summed = lax.all_to_all(term, "zh", 0, 0, tiled=True)
    factors, sensed = fenced(beside_sums, *inputs)

    summed = jnp.sum(summed.astype(jnp.float32), axis=0)
    active = [
        (jax.nn.silu(summed[:, at : at + cols]) * summed[:, at + cols : at + 2 * cols]).astype(jnp.bfloat16)
        for at in (0, 2 * cols)
    ]
    active = in_order(*active, c, 1)
    active, factors, sensed = lax.optimization_barrier((active, factors, sensed))
    active = in_order(active, lax.ppermute(active, "c", SWAP), c, 0)
    projected = lax.dot_general(factors, active, (((1,), (1,)), ((), ())), preferred_element_type=jnp.float32)

    parts = [v.reshape(chips, rank, tokens) for v in (projected.astype(jnp.bfloat16), sensed)]
    parts = lax.all_to_all(jnp.concatenate(parts, axis=1), CHIPS, 0, 0, tiled=True)
    whole = jnp.sum(parts.astype(jnp.float32), axis=0)
    return jnp.sum(whole[:rank] * whole[rank:], axis=0, keepdims=True)


def solution(mesh):
    torus = Mesh(mesh.devices.reshape(8, 2, 2, 4, 2, 2), ("y", "xl", "xh", "zh", "zl", "c"))
    placed = (
        P(TRAIN, None),
        P(),
        P(TRAIN, QM),
        P(TRAIN, QM),
        P(TRAIN, QM),
        P(QM, None, None),
        P(QM, None, None),
    )
    return jax.shard_map(on_device, mesh=torus, in_specs=placed, out_specs=P(QM, TRAIN), check_vma=False)
```

```python
import jax
import jax.numpy as jnp
from jax import lax
from jax.experimental import pallas as pl
from jax.experimental.pallas import tpu as pltpu
from jax.sharding import Mesh
from jax.sharding import PartitionSpec as P

TRAIN = ("xh", "zh", "zl")
DEPTH = ("zh", "zl")
QM = ("y", "xl", "c")
CHIPS = ("y", "xl")
SWAP = ((0, 1), (1, 0))
RING = 8
STEPS = RING // 2 + 1
EARLY = (2, 3, 1)


def away(step, xh):
    sign = 1 if step == 3 else -1
    return step if step in (0, RING // 2) else sign * step * (1 - 2 * xh)


norm_eps = 1e-05


def norm_kernel(core_ref, pair_ref, own_ref, other_ref, own_gain_ref, other_gain_ref, out_ref):
    halves = [ref[...].astype(jnp.float32) for ref in (own_ref, other_ref)]
    gains = [ref[...] for ref in (own_gain_ref, other_gain_ref)]
    peers, _, width = out_ref.shape
    square = sum(jnp.sum(h * h, axis=1, keepdims=True) for h in halves)
    scale = lax.rsqrt(square / (peers * width) + norm_eps)
    rows = width // 2
    for part in range(2):
        normed = (halves[part] * scale * gains[part]).astype(out_ref.dtype)
        for k in range(peers):
            out_ref[k, :, part * rows : (part + 1) * rows] = normed[:, k * rows : (k + 1) * rows]


def normed_by_peer(residual, norm_gain, core, pair, peers):
    tokens, width = residual.shape
    mine, slab = tokens // 2, 32
    steps = mine // slab
    gain = norm_gain.reshape(1, width)
    return pl.pallas_call(
        norm_kernel,
        out_shape=jax.ShapeDtypeStruct((peers, mine, width // peers), jnp.bfloat16),
        grid_spec=pltpu.PrefetchScalarGridSpec(
            num_scalar_prefetch=2,
            grid=(steps,),
            in_specs=[
                pl.BlockSpec((slab, width // 2), lambda i, c, x: (c[0] * steps + i, x[0])),
                pl.BlockSpec((slab, width // 2), lambda i, c, x: (c[0] * steps + i, 1 - x[0])),
                pl.BlockSpec((1, width // 2), lambda i, c, x: (0, x[0])),
                pl.BlockSpec((1, width // 2), lambda i, c, x: (0, 1 - x[0])),
            ],
            out_specs=pl.BlockSpec((peers, slab, width // peers), lambda i, c, x: (0, i, 0)),
        ),
        compiler_params=pltpu.CompilerParams(vmem_limit_bytes=60 << 20),
        cost_estimate=pl.CostEstimate(flops=4 * mine * width, bytes_accessed=4 * mine * width, transcendentals=mine),
        name="norm_rows",
    )(core.reshape(1), pair.reshape(1), residual, residual, gain, gain)


def term_kernel(parity_ref, rows_ref, weight_ref, out_ref):
    peers, half, width = rows_ref.shape
    rows = jnp.concatenate([rows_ref[2 * i + parity_ref[0]] for i in range(peers // 2)], axis=0)
    cols = weight_ref.shape[0] // 2
    for core in range(2):
        at = slice(core * cols, (core + 1) * cols)
        total = lax.dot_general(rows, weight_ref[at], (((1,), (1,)), ((), ())), preferred_element_type=jnp.float32)
        out_ref[:, :, at] = total.astype(out_ref.dtype).reshape(peers // 2, half, cols)


def terms_of(rows, weight, parity, kind):
    peers, half, width = rows.shape
    cols = weight.shape[0]
    shape = jax.ShapeDtypeStruct((peers // 2, half, cols), kind)
    return whole_kernel(term_kernel, (parity,), (rows, weight), [shape], "terms", peers * half * width * cols)[0]


def add_kernel(keep_ref, got_ref, out_ref):
    out_ref[...] = (keep_ref[...] + got_ref[...].astype(jnp.float32)).astype(out_ref.dtype)


def whole_kernel(body, scalars, inputs, outputs, name, flops=0):
    size = sum(v.size * v.dtype.itemsize for v in (*inputs, *outputs))
    vmem = pl.BlockSpec(memory_space=pltpu.VMEM)
    return pl.pallas_call(
        body,
        out_shape=outputs,
        in_specs=[pl.BlockSpec(memory_space=pltpu.SMEM)] * len(scalars) + [vmem] * len(inputs),
        out_specs=[vmem] * len(outputs),
        compiler_params=pltpu.CompilerParams(vmem_limit_bytes=24 << 20),
        cost_estimate=pl.CostEstimate(flops=flops, bytes_accessed=size, transcendentals=0),
        name=name,
    )(*(v.reshape(1) for v in scalars), *inputs)


def weight_kernel(mine_ref, theirs_ref, beside_ref, across_ref, out_ref):
    cols, depth = mine_ref.shape
    for row, refs in enumerate(((mine_ref, theirs_ref), (beside_ref, across_ref))):
        for col, ref in enumerate(refs):
            out_ref[row * cols : (row + 1) * cols, col * depth : (col + 1) * depth] = ref[...]


def pack_kernel(y_ref, xh_ref, left_ref, right_ref, *out_refs):
    rank, hidden = left_ref.shape[0], left_ref.shape[1] // (2 * RING)
    features = right_ref.shape[1] // (2 * RING)
    for step, out_ref in enumerate(out_refs):
        to = lax.rem(y_ref[0] + RING + away(step, xh_ref[0]), RING)
        for xl in range(2):
            at = pl.multiple_of((to * 2 + xl) * hidden, 128)
            out_ref[xl, :, :hidden] = left_ref[:, pl.ds(at, hidden)]
            at = pl.multiple_of((to * 2 + xl) * features, 128)
            out_ref[xl, :, hidden:] = right_ref[:, pl.ds(at, features)]


def give_kernel(xl_ref, *refs):
    arrived, (aside_ref, across_ref, apart_ref) = refs[:-3], refs[-3:]
    xl = xl_ref[0]
    for step, ref in enumerate(arrived):
        aside_ref[step] = ref[1 - xl]
        if step > 0:
            across_ref[step - 1] = ref[xl]
            apart_ref[step - 1] = ref[1 - xl]


def gather_kernel(c_ref, xl_ref, y_ref, xh_ref, *refs):
    arrived, refs = refs[:STEPS], refs[STEPS:]
    aside_ref, far_ref, across_ref, apart_ref, grad_ref, beside_ref, left_ref, sensed_ref, right_ref = refs
    hidden = left_ref.shape[-1]
    xl = xl_ref[0]
    for step, ref in enumerate(arrived):
        source = lax.rem(y_ref[0] + RING - away(step, xh_ref[0]), RING)
        found = [(source, xl, ref[xl]), (source, 1 - xl, (aside_ref[step] if step < STEPS - 1 else far_ref[...]))]
        if 0 < step < STEPS - 1:
            source = lax.rem(y_ref[0] + RING + away(step, xh_ref[0]), RING)
            found += [(source, xl, across_ref[step - 1]), (source, 1 - xl, apart_ref[step - 1])]
        for source, at, value in found:
            left_ref[source, at] = value[:, :hidden]
            right_ref[source, at] = value[:, hidden:]
    ring, _, rank, features = right_ref.shape
    total = jnp.zeros(sensed_ref.shape, jnp.float32)
    for core, ref in ((c_ref[0], grad_ref), (1 - c_ref[0], beside_ref)):
        at = pl.ds(pl.multiple_of(core * (features // 2), 128), features // 2)
        factor = right_ref[:, :, :, at].reshape(2 * ring * rank, features // 2)
        total += lax.dot_general(factor, ref[...], (((1,), (1,)), ((), ())), preferred_element_type=jnp.float32)
    sensed_ref[...] = total.astype(sensed_ref.dtype)


def in_order(own, other, index, dim):
    return jnp.concatenate([jnp.where(index == 0, own, other), jnp.where(index == 0, other, own)], axis=dim)


def on_device(residual, norm_gain, gate_weight, up_weight, out_grad, left_factor, right_factor):
    c, xh, xl, y, zl = (lax.axis_index(name) for name in ("c", "xh", "xl", "y", "zl"))
    peers, chips = lax.axis_size(DEPTH), lax.axis_size(CHIPS)
    tokens = residual.shape[0]
    cols = gate_weight.shape[1]
    rank = left_factor.shape[1]
    hidden, features = left_factor.shape[2] // chips, right_factor.shape[2] // chips
    packed = hidden + features
    always = c >= 0

    def fenced(work, *inputs):
        shapes = jax.eval_shape(work, *inputs)
        return lax.cond(always, work, lambda *_: jax.tree.map(lambda s: jnp.zeros(s.shape, s.dtype), shapes), *inputs)

    def like(*shape):
        return jax.ShapeDtypeStruct(shape, jnp.bfloat16)

    def along_y(piece, step):
        pairs = [(i * 2 + h, (i + RING + away(step, h)) % RING * 2 + h) for i in range(RING) for h in range(2)]
        return lax.ppermute(piece, ("y", "xh"), pairs)

    def beside_tokens(gate_weight, up_weight, out_grad, left_factor, right_factor):
        mine = jnp.concatenate([gate_weight.T, up_weight.T], axis=0)
        theirs = lax.ppermute(mine, "xh", SWAP)
        pieces = whole_kernel(
            pack_kernel, (y, xh), (left_factor[0], right_factor[0]), [like(2, rank, packed)] * STEPS, "pack_factors"
        )
        early = tuple(along_y(pieces[step], step) for step in EARLY)
        theirs, early = lax.optimization_barrier((theirs, early))
        beside = (lax.ppermute(mine, "c", SWAP), lax.ppermute(theirs, "c", SWAP))
        (weight,) = whole_kernel(
            weight_kernel, (), (mine, theirs, *beside), [like(4 * cols, 2 * gate_weight.shape[0])], "weights"
        )
        late = (pieces[0], pieces[STEPS - 1])
        return weight, early, late, lax.ppermute(out_grad, "c", SWAP)

    def beside_sums(near, far, out_grad, beside_grad):
        pieces = [like(STEPS - 1, rank, packed)] + [like(STEPS - 2, rank, packed)] * 2
        aside, across, apart = whole_kernel(give_kernel, (xl,), near, pieces, "give")
        across = lax.ppermute(across, "xh", SWAP)
        apart = lax.ppermute(apart, ("xl", "xh"), [(i, 3 - i) for i in range(4)])
        aside = lax.ppermute(aside, "xl", SWAP)
        beyond = lax.ppermute(lax.dynamic_index_in_dim(far, 1 - xl, 0, keepdims=False), "xl", SWAP)
        outputs = [like(RING, 2, rank, hidden), like(chips * rank, tokens), like(RING, 2, rank, features)]
        inputs = (*near, far, aside, beyond, across, apart, out_grad, beside_grad)
        left, sensed, _ = whole_kernel(gather_kernel, (c, xl, y, xh), inputs, outputs, "gather_factors")
        return left.reshape(chips * rank, hidden), sensed

    normed = normed_by_peer(residual, norm_gain, c, xh, peers)
    inputs, normed = lax.optimization_barrier(((gate_weight, up_weight, out_grad, left_factor, right_factor), normed))
    rows = lax.all_to_all(normed, DEPTH, 0, 0, tiled=True)
    weight, early, late, beside_grad = fenced(beside_tokens, *inputs)

    give = terms_of(rows, weight, 1 - zl, jnp.bfloat16)
    give, rows = lax.optimization_barrier((give, rows))
    pairs = []
    for z in range(peers):
        for core in range(2):
            side = 1 if z % 2 == core else -1
            pairs.append((z * 2 + core, (z + side) % peers * 2 + core))
    got = lax.ppermute(give, DEPTH + ("c",), pairs)
    keep = terms_of(rows, weight, zl, jnp.float32)
    late, give = lax.optimization_barrier((late, give))
    far = along_y(late[1], STEPS - 1)
    near = [late[0]] + [early[EARLY.index(step)] for step in range(1, STEPS - 1)]
    (term,) = whole_kernel(add_kernel, (), (keep, got), [like(peers // 2, tokens // 2, 4 * cols)], "add_terms")
    inputs, term = lax.optimization_barrier(((near, far, out_grad, beside_grad), term))
    summed = lax.all_to_all(term, "zh", 0, 0, tiled=True)
    factors, sensed = fenced(beside_sums, *inputs)

    summed = jnp.sum(summed.astype(jnp.float32), axis=0)
    active = [
        (jax.nn.silu(summed[:, at : at + cols]) * summed[:, at + cols : at + 2 * cols]).astype(jnp.bfloat16)
        for at in (0, 2 * cols)
    ]
    active = in_order(*active, c, 1)
    active, factors, sensed = lax.optimization_barrier((active, factors, sensed))
    active = in_order(active, lax.ppermute(active, "c", SWAP), c, 0)
    projected = lax.dot_general(factors, active, (((1,), (1,)), ((), ())), preferred_element_type=jnp.float32)

    parts = [v.reshape(chips, rank, tokens) for v in (projected.astype(jnp.bfloat16), sensed)]
    parts = lax.all_to_all(jnp.concatenate(parts, axis=1), CHIPS, 0, 0, tiled=True)
    whole = jnp.sum(parts.astype(jnp.float32), axis=0)
    return jnp.sum(whole[:rank] * whole[rank:], axis=0, keepdims=True)


def solution(mesh):
    torus = Mesh(mesh.devices.reshape(8, 2, 2, 4, 2, 2), ("y", "xl", "xh", "zh", "zl", "c"))
    placed = (
        P(TRAIN, None),
        P(),
        P(TRAIN, QM),
        P(TRAIN, QM),
        P(TRAIN, QM),
        P(QM, None, None),
        P(QM, None, None),
    )
    return jax.shard_map(on_device, mesh=torus, in_specs=placed, out_specs=P(QM, TRAIN), check_vma=False)
```

```python
import jax
import jax.numpy as jnp
from jax import lax
from jax.experimental import pallas as pl
from jax.experimental.pallas import tpu as pltpu
from jax.sharding import Mesh
from jax.sharding import PartitionSpec as P

TRAIN = ("xh", "zh", "zl")
DEPTH = ("zh", "zl")
QM = ("y", "xl", "c")
CHIPS = ("y", "xl")
SWAP = ((0, 1), (1, 0))
RING = 8
STEPS = RING // 2 + 1
EARLY = (2, 3, 1)


def away(step, xh):
    sign = 1 if step == 3 else -1
    return step if step in (0, RING // 2) else sign * step * (1 - 2 * xh)


norm_eps = 1e-05


def norm_kernel(core_ref, pair_ref, own_ref, other_ref, own_gain_ref, other_gain_ref, out_ref):
    halves = [ref[...].astype(jnp.float32) for ref in (own_ref, other_ref)]
    gains = [ref[...] for ref in (own_gain_ref, other_gain_ref)]
    peers, _, width = out_ref.shape
    square = sum(jnp.sum(h * h, axis=1, keepdims=True) for h in halves)
    scale = lax.rsqrt(square / (peers * width) + norm_eps)
    rows = width // 2
    for part in range(2):
        normed = (halves[part] * scale * gains[part]).astype(out_ref.dtype)
        for k in range(peers):
            out_ref[k, :, part * rows : (part + 1) * rows] = normed[:, k * rows : (k + 1) * rows]


def normed_by_peer(residual, norm_gain, core, pair, peers):
    tokens, width = residual.shape
    mine, slab = tokens // 2, 32
    steps = mine // slab
    gain = norm_gain.reshape(1, width)
    return pl.pallas_call(
        norm_kernel,
        out_shape=jax.ShapeDtypeStruct((peers, mine, width // peers), jnp.bfloat16),
        grid_spec=pltpu.PrefetchScalarGridSpec(
            num_scalar_prefetch=2,
            grid=(steps,),
            in_specs=[
                pl.BlockSpec((slab, width // 2), lambda i, c, x: (c[0] * steps + i, x[0])),
                pl.BlockSpec((slab, width // 2), lambda i, c, x: (c[0] * steps + i, 1 - x[0])),
                pl.BlockSpec((1, width // 2), lambda i, c, x: (0, x[0])),
                pl.BlockSpec((1, width // 2), lambda i, c, x: (0, 1 - x[0])),
            ],
            out_specs=pl.BlockSpec((peers, slab, width // peers), lambda i, c, x: (0, i, 0)),
        ),
        compiler_params=pltpu.CompilerParams(vmem_limit_bytes=60 << 20),
        cost_estimate=pl.CostEstimate(flops=4 * mine * width, bytes_accessed=4 * mine * width, transcendentals=mine),
        name="norm_rows",
    )(core.reshape(1), pair.reshape(1), residual, residual, gain, gain)


def term_kernel(parity_ref, rows_ref, weight_ref, beside_ref, out_ref, beside_vmem, sem):
    copy = pltpu.make_async_copy(beside_ref, beside_vmem, sem)
    copy.start()
    peers, half, width = rows_ref.shape
    rows = jnp.concatenate([rows_ref[2 * i + parity_ref[0]] for i in range(peers // 2)], axis=0)
    cols = weight_ref.shape[0]
    for core, ref in enumerate((weight_ref, beside_vmem)):
        if core:
            copy.wait()
        total = lax.dot_general(rows, ref[...], (((1,), (1,)), ((), ())), preferred_element_type=jnp.float32)
        total = total.astype(out_ref.dtype).reshape(peers // 2, half, cols)
        out_ref[:, :, core * cols : (core + 1) * cols] = total


def terms_of(rows, weights, parity):
    peers, half, width = rows.shape
    cols = weights[0].shape[0]
    vmem = pl.BlockSpec(memory_space=pltpu.VMEM)
    return pl.pallas_call(
        term_kernel,
        out_shape=jax.ShapeDtypeStruct((peers // 2, half, 2 * cols), jnp.bfloat16),
        in_specs=[pl.BlockSpec(memory_space=pltpu.SMEM), vmem, vmem, pl.BlockSpec(memory_space=pl.ANY)],
        out_specs=vmem,
        scratch_shapes=[pltpu.VMEM(weights[1].shape, jnp.bfloat16), pltpu.SemaphoreType.DMA(())],
        compiler_params=pltpu.CompilerParams(vmem_limit_bytes=24 << 20),
        cost_estimate=pl.CostEstimate(
            flops=2 * peers * half * width * cols, bytes_accessed=6 * peers * half * width, transcendentals=0
        ),
        name="terms",
    )(parity.reshape(1), rows, *weights)


def add_kernel(keep_ref, got_ref, out_ref):
    out_ref[...] = (keep_ref[...].astype(jnp.float32) + got_ref[...].astype(jnp.float32)).astype(out_ref.dtype)


def whole_kernel(body, scalars, inputs, outputs, name, flops=0):
    size = sum(v.size * v.dtype.itemsize for v in (*inputs, *outputs))
    vmem = pl.BlockSpec(memory_space=pltpu.VMEM)
    return pl.pallas_call(
        body,
        out_shape=outputs,
        in_specs=[pl.BlockSpec(memory_space=pltpu.SMEM)] * len(scalars) + [vmem] * len(inputs),
        out_specs=[vmem] * len(outputs),
        compiler_params=pltpu.CompilerParams(vmem_limit_bytes=24 << 20),
        cost_estimate=pl.CostEstimate(flops=flops, bytes_accessed=size, transcendentals=0),
        name=name,
    )(*(v.reshape(1) for v in scalars), *inputs)


def weight_kernel(own_ref, partner_ref, out_ref):
    depth = own_ref.shape[1]
    out_ref[:, :depth] = own_ref[...]
    out_ref[:, depth:] = partner_ref[...]


def pack_kernel(y_ref, xh_ref, left_ref, right_ref, *out_refs):
    rank, hidden = left_ref.shape[0], left_ref.shape[1] // (2 * RING)
    features = right_ref.shape[1] // (2 * RING)
    for step, out_ref in enumerate(out_refs):
        to = lax.rem(y_ref[0] + RING + away(step, xh_ref[0]), RING)
        for xl in range(2):
            at = pl.multiple_of((to * 2 + xl) * hidden, 128)
            out_ref[xl, :, :hidden] = left_ref[:, pl.ds(at, hidden)]
            at = pl.multiple_of((to * 2 + xl) * features, 128)
            out_ref[xl, :, hidden:] = right_ref[:, pl.ds(at, features)]


def give_kernel(xl_ref, *refs):
    arrived, (aside_ref, across_ref, apart_ref) = refs[:-3], refs[-3:]
    xl = xl_ref[0]
    for step, ref in enumerate(arrived):
        aside_ref[step] = ref[1 - xl]
        if step > 0:
            across_ref[step - 1] = ref[xl]
            apart_ref[step - 1] = ref[1 - xl]


def gather_kernel(c_ref, xl_ref, y_ref, xh_ref, *refs):
    arrived, refs = refs[:STEPS], refs[STEPS:]
    aside_ref, far_ref, across_ref, apart_ref, grad_ref, beside_ref, left_ref, sensed_ref, right_ref = refs
    hidden = left_ref.shape[-1]
    xl = xl_ref[0]
    for step, ref in enumerate(arrived):
        source = lax.rem(y_ref[0] + RING - away(step, xh_ref[0]), RING)
        found = [(source, xl, ref[xl]), (source, 1 - xl, (aside_ref[step] if step < STEPS - 1 else far_ref[...]))]
        if 0 < step < STEPS - 1:
            source = lax.rem(y_ref[0] + RING + away(step, xh_ref[0]), RING)
            found += [(source, xl, across_ref[step - 1]), (source, 1 - xl, apart_ref[step - 1])]
        for source, at, value in found:
            left_ref[source, at] = value[:, :hidden]
            right_ref[source, at] = value[:, hidden:]
    ring, _, rank, features = right_ref.shape
    total = jnp.zeros(sensed_ref.shape, jnp.float32)
    for core, ref in ((c_ref[0], grad_ref), (1 - c_ref[0], beside_ref)):
        at = pl.ds(pl.multiple_of(core * (features // 2), 128), features // 2)
        factor = right_ref[:, :, :, at].reshape(2 * ring * rank, features // 2)
        total += lax.dot_general(factor, ref[...], (((1,), (1,)), ((), ())), preferred_element_type=jnp.float32)
    sensed_ref[...] = total.astype(sensed_ref.dtype)


def in_order(own, other, index, dim):
    return jnp.concatenate([jnp.where(index == 0, own, other), jnp.where(index == 0, other, own)], axis=dim)


def on_device(residual, norm_gain, gate_weight, up_weight, out_grad, left_factor, right_factor):
    c, xh, xl, y, zl = (lax.axis_index(name) for name in ("c", "xh", "xl", "y", "zl"))
    peers, chips = lax.axis_size(DEPTH), lax.axis_size(CHIPS)
    tokens = residual.shape[0]
    cols = gate_weight.shape[1]
    rank = left_factor.shape[1]
    hidden, features = left_factor.shape[2] // chips, right_factor.shape[2] // chips
    packed = hidden + features
    always = c >= 0

    def fenced(work, *inputs):
        shapes = jax.eval_shape(work, *inputs)
        return lax.cond(always, work, lambda *_: jax.tree.map(lambda s: jnp.zeros(s.shape, s.dtype), shapes), *inputs)

    def like(*shape):
        return jax.ShapeDtypeStruct(shape, jnp.bfloat16)

    def along_y(piece, step):
        pairs = [(i * 2 + h, (i + RING + away(step, h)) % RING * 2 + h) for i in range(RING) for h in range(2)]
        return lax.ppermute(piece, ("y", "xh"), pairs)

    def beside_tokens(gate_weight, up_weight, out_grad, left_factor, right_factor):
        mine = jnp.concatenate([gate_weight.T, up_weight.T], axis=0)
        theirs = lax.ppermute(mine, "xh", SWAP)
        pieces = whole_kernel(
            pack_kernel, (y, xh), (left_factor[0], right_factor[0]), [like(2, rank, packed)] * STEPS, "pack_factors"
        )
        early = tuple(along_y(pieces[step], step) for step in EARLY)
        theirs, early = lax.optimization_barrier((theirs, early))
        beside = (lax.ppermute(mine, "c", SWAP), lax.ppermute(theirs, "c", SWAP))
        shape = like(2 * cols, 2 * gate_weight.shape[0])
        weights = [whole_kernel(weight_kernel, (), pair, [shape], "weights")[0] for pair in ((mine, theirs), beside)]
        late = (pieces[0], pieces[STEPS - 1])
        return weights, early, late, lax.ppermute(out_grad, "c", SWAP)

    def beside_sums(near, far, out_grad, beside_grad):
        pieces = [like(STEPS - 1, rank, packed)] + [like(STEPS - 2, rank, packed)] * 2
        aside, across, apart = whole_kernel(give_kernel, (xl,), near, pieces, "give")
        across = lax.ppermute(across, "xh", SWAP)
        apart = lax.ppermute(apart, ("xl", "xh"), [(i, 3 - i) for i in range(4)])
        aside = lax.ppermute(aside, "xl", SWAP)
        beyond = lax.ppermute(lax.dynamic_index_in_dim(far, 1 - xl, 0, keepdims=False), "xl", SWAP)
        outputs = [like(RING, 2, rank, hidden), like(chips * rank, tokens), like(RING, 2, rank, features)]
        inputs = (*near, far, aside, beyond, across, apart, out_grad, beside_grad)
        left, sensed, _ = whole_kernel(gather_kernel, (c, xl, y, xh), inputs, outputs, "gather_factors")
        return left.reshape(chips * rank, hidden), sensed

    normed = normed_by_peer(residual, norm_gain, c, xh, peers)
    inputs, normed = lax.optimization_barrier(((gate_weight, up_weight, out_grad, left_factor, right_factor), normed))
    rows = lax.all_to_all(normed, DEPTH, 0, 0, tiled=True)
    weights, early, late, beside_grad = fenced(beside_tokens, *inputs)

    give = terms_of(rows, weights, 1 - zl)
    give, rows = lax.optimization_barrier((give, rows))
    pairs = []
    for z in range(peers):
        for core in range(2):
            side = 1 if z % 2 == core else -1
            pairs.append((z * 2 + core, (z + side) % peers * 2 + core))
    got = lax.ppermute(give, DEPTH + ("c",), pairs)
    keep = terms_of(rows, weights, zl)
    late, give = lax.optimization_barrier((late, give))
    far = along_y(late[1], STEPS - 1)
    near = [late[0]] + [early[EARLY.index(step)] for step in range(1, STEPS - 1)]
    (term,) = whole_kernel(add_kernel, (), (keep, got), [like(peers // 2, tokens // 2, 4 * cols)], "add_terms")
    inputs, term = lax.optimization_barrier(((near, far, out_grad, beside_grad), term))
    summed = lax.all_to_all(term, "zh", 0, 0, tiled=True)
    factors, sensed = fenced(beside_sums, *inputs)

    summed = jnp.sum(summed.astype(jnp.float32), axis=0)
    active = [
        (jax.nn.silu(summed[:, at : at + cols]) * summed[:, at + cols : at + 2 * cols]).astype(jnp.bfloat16)
        for at in (0, 2 * cols)
    ]
    active = in_order(*active, c, 1)
    active, factors, sensed = lax.optimization_barrier((active, factors, sensed))
    active = in_order(active, lax.ppermute(active, "c", SWAP), c, 0)
    projected = lax.dot_general(factors, active, (((1,), (1,)), ((), ())), preferred_element_type=jnp.float32)

    parts = [v.reshape(chips, rank, tokens) for v in (projected.astype(jnp.bfloat16), sensed)]
    parts = lax.all_to_all(jnp.concatenate(parts, axis=1), CHIPS, 0, 0, tiled=True)
    whole = jnp.sum(parts.astype(jnp.float32), axis=0)
    return jnp.sum(whole[:rank] * whole[rank:], axis=0, keepdims=True)


def solution(mesh):
    torus = Mesh(mesh.devices.reshape(8, 2, 2, 4, 2, 2), ("y", "xl", "xh", "zh", "zl", "c"))
    placed = (
        P(TRAIN, None),
        P(),
        P(TRAIN, QM),
        P(TRAIN, QM),
        P(TRAIN, QM),
        P(QM, None, None),
        P(QM, None, None),
    )
    return jax.shard_map(on_device, mesh=torus, in_specs=placed, out_specs=P(QM, TRAIN), check_vma=False)
```
